128 devices in a mesh: row: 32 (over y, z, core), col: 4 (over x).
Axes of the slice: x: 4, y: 4, z: 4, core: 2. Of those that a mesh axis runs over, the one named last changes fastest.
Arguments:
- disk: bfloat16 [16, 4096, 2048], P(None, 'row', 'col'), may hold values from -6 to 6
- response: bfloat16 [19, 19], replicated, may hold values from -0.3125 to 0.3125
- spectra: bfloat16 [2048, 196608], P('col', 'row'), may hold values from -6 to 6
- srf: bfloat16 [16, 2048], P(None, 'col'), may hold values from -0.125 to 0.125
- send_pix: int32 [4718592], P(('row', 'col')), may hold values from 0 to 65535, as said below
- recv_foot: int32 [4718592], P(('row', 'col')), may hold values from 0 to 1536, as said below
Outputs:
- blurred: bfloat16 [16, 4096, 2048], P(None, 'row', 'col')
- mismatch: float32 [16, 196608], P(None, ('row', 'col'))
The draws below stay inside these ranges and needn't reach their ends.
Inputs may be any that keep to these rules, and one draw needn't show every extreme that they name: `send_pix`: every value is a local pixel offset in the sending tile, row * 512 + column. `recv_foot`: within each receiving device's 128 * 288 slots, every one of its 1536 footprints is named exactly 16 times; 1536 marks a slot that carries nothing; for each receiving device some sending tile fills all 288 of its slots.
All inputs are finite; a program needn't handle non-finite values.
Results may differ from the reference program's by a relative error of at most 0.001.
Values may be sent and summed in bfloat16 or wider, within the bound.
A program may use at most 128 MiB of HBM per device.

```python
import jax
import jax.numpy as jnp
from jax import lax

BANDS = 16
CH = 2048
KS = 19
NSAMP = 16
TR = 128
TC = 512
FPD = 1536
SENDERS = 128
CAP = 288
H = 4096
W = 2048
FOOTPRINTS = 196608
N_COL = 4


def collocation_tables(key):
    slot_count = SENDERS * CAP
    live_count = FPD * NSAMP

    def for_target(target):
        base = jax.random.fold_in(jax.random.fold_in(key, 7101), target)
        key_hot, key_order, key_items, key_pixel, key_top = jax.random.split(base, 5)
        hottest = jax.random.randint(key_hot, (), 0, SENDERS)
        priority = jax.random.permutation(key_order, slot_count).astype(jnp.int32)
        source = jnp.arange(slot_count, dtype=jnp.int32) // CAP
        priority = jnp.where(source == hottest, priority - slot_count, priority)
        ordering = jnp.argsort(priority, stable=True)
        ranking = jnp.zeros((slot_count,), jnp.int32).at[ordering].set(jnp.arange(slot_count, dtype=jnp.int32))
        items = jax.random.permutation(key_items, live_count).astype(jnp.int32)
        picked = items[jnp.minimum(ranking, live_count - 1)] // NSAMP
        owners = jnp.where(ranking < live_count, picked, FPD).astype(jnp.int32)
        pixels = jax.random.randint(key_pixel, (slot_count,), 0, TR * TC).astype(jnp.int32)
        top_place = jax.random.randint(key_top, (), 0, slot_count)
        pixels = pixels.at[top_place].set(TR * TC - 1)
        pixels = pixels.at[(top_place + 1) % slot_count].set(0)
        return (owners, pixels)
    return jax.vmap(for_target)(jnp.arange(SENDERS, dtype=jnp.int32))


def draw_recv_foot(key, part):
    owners, pixels = collocation_tables(key)
    return owners.reshape(-1).astype(jnp.int32)


def draw_send_pix(key, part):
    owners, pixels = collocation_tables(key)
    table = pixels.reshape(SENDERS, SENDERS, CAP)
    return jnp.transpose(table, (1, 0, 2)).reshape(-1).astype(jnp.int32)


def block_scale(own_key, shape, shards, smallest, largest):
    level, own = 1.0, jax.random.fold_in(own_key, 6)
    for dim, blocks in shards:
        steps = jnp.exp(jax.random.uniform(jax.random.fold_in(own, dim), (blocks,), jnp.float32, smallest / len(shards), largest / len(shards)))
        level = level * jnp.repeat(steps, shape[dim] // blocks).reshape([-1 if axis == dim else 1 for axis in range(len(shape))])
    return level


def scatter_about(rng, shape, width, bound, cuts=(), kind=jnp.bfloat16):
    drawn = width * jax.random.normal(rng, shape, jnp.float32)
    if cuts:
        drawn = drawn * block_scale(rng, shape, cuts, -0.22, 0.18)
    return jnp.clip(drawn, -bound, bound).astype(kind)


def setup_inputs(seed: int = 0) -> dict:
    arg_keys = jax.random.split(jax.random.key(seed), 7)
    return {
        "disk": scatter_about(arg_keys[0], (BANDS, H, W), 1.0, 6.0, ((1, 32), (2, 4))),
        "response": scatter_about(arg_keys[1], (KS, KS), (KS * KS) ** -0.5, 0.3125),
        "spectra": scatter_about(arg_keys[2], (CH, FOOTPRINTS), 1.0, 6.0, ((0, 4), (1, 32))),
        "srf": scatter_about(arg_keys[3], (BANDS, CH), CH ** -0.5, 0.125, ((1, 4),)),
        "send_pix": draw_send_pix(jax.random.fold_in(arg_keys[6], 71), 0),
        "recv_foot": draw_recv_foot(jax.random.fold_in(arg_keys[6], 71), 0),
    }


def reference(disk, response, spectra, srf, send_pix, recv_foot):
    margin = KS // 2
    kernel = response.astype(jnp.float32)[None, None]

    def blur_plane(plane):
        result = lax.conv_general_dilated(plane.astype(jnp.float32)[None, None], kernel, (1, 1), ((margin, margin), (margin, margin)), precision=lax.Precision.HIGHEST)
        return result[0, 0].astype(jnp.bfloat16)

    blurred = lax.map(blur_plane, disk)
    evolved = jnp.dot(srf, spectra, preferred_element_type=jnp.float32)
    flat_disk = blurred.reshape(BANDS, H * W)
    send_table = send_pix.reshape(SENDERS, SENDERS, CAP)
    recv_table = recv_foot.reshape(SENDERS, SENDERS, CAP)
    sources = jnp.arange(SENDERS, dtype=jnp.int32)
    corner = (sources // N_COL) * TR * W + (sources % N_COL) * TC

    def one_dest(target):
        offsets = send_table[:, target, :]
        places = corner[:, None] + (offsets // TC) * W + offsets % TC
        values = jnp.take(flat_disk, places.reshape(-1), axis=1).astype(jnp.float32)
        owners = recv_table[target].reshape(-1)
        totals = jax.ops.segment_sum(values.T, owners, num_segments=FPD + 1)
        return totals[:FPD].T

    imager = lax.map(one_dest, sources)
    imager = jnp.transpose(imager, (1, 0, 2)).reshape(BANDS, FOOTPRINTS) / NSAMP
    return blurred, evolved - imager
```

```python
import functools

import jax
import jax.numpy as jnp
import numpy as np
from jax import lax
from jax.experimental import pallas as pl
from jax.experimental.pallas import tpu as pltpu
from jax.sharding import PartitionSpec as P

NSAMP = 16
BANDS = 16
KS = 19
TR = 128
TC = 512
FPD = 1536
ND = 128
CAP = 288
N_COL = 4
UNITS = 8
ROWS = CAP // UNITS
PADR = 40
QUART = 4
PERQ = ND // QUART
CELLS = TR // 8 * TC
HI = FPD // 128
MESH = pl.DeviceIdType.MESH


def blur_kernel(p_ref, w_ref, out_ref, tab_ref, s_ref):
    def block(yb, carry):
        acc = None
        for a in range(KS + 1):
            left = jnp.concatenate(
                [
                    p_ref[pl.ds(yb * 8 + a // 2, 8), a % 2, :, j * 128 : j * 128 + 256].reshape(128, 256)
                    for j in range(4)
                ],
                axis=0,
            )
            right = jnp.concatenate([w_ref[a + 1], w_ref[a]], axis=1)
            term = jnp.dot(left, right, preferred_element_type=jnp.float32)
            acc = term if acc is None else acc + term
        rounded = acc.astype(jnp.bfloat16).astype(jnp.float32)
        for j in range(4):
            rows = [
                rounded[j * 128 + m * 16 : j * 128 + m * 16 + 16, q * 128 : q * 128 + 128]
                for m in range(8)
                for q in range(2)
            ]
            for h in range(2):
                piece = jnp.concatenate(rows[8 * h : 8 * h + 8], axis=0)
                s_ref[j, pl.ds(h * 128, 128), :] = piece
                at = pl.multiple_of((2 * yb + h) * TC + j * 128, 128)
                tab_ref[pl.ds(at, 128), :] = jnp.transpose(piece)
            for b in range(BANDS):
                out_ref[b, pl.ds(pl.multiple_of(yb * 16, 16), 16), j * 128 : j * 128 + 128] = s_ref[
                    j, pl.ds(b, 16, stride=16), :
                ].astype(jnp.bfloat16)
        return carry

    lax.fori_loop(0, TR // 16, block, 0)


def collect_kernel(
    idx_ref, tab_ref, foot_ref, out_ref, rot, stage, send, recv, wide, acc, send_sem, recv_sem
):
    me = lax.axis_index("row") * N_COL + lax.axis_index("col")
    mq = me // PERQ
    ml = lax.rem(me, PERQ)

    barrier = pltpu.get_barrier_semaphore()

    def greet(i, carry):
        other = lax.rem(me + i, ND)
        pl.semaphore_signal(
            barrier, inc=1, device_id=(other // N_COL, lax.rem(other, N_COL)), device_id_type=MESH
        )
        return carry

    lax.fori_loop(1, ND, greet, 0)

    def turn(i, carry):
        cells = tab_ref[pl.ds(pl.multiple_of(i * 128, 128), 128), :]
        for j in range(UNITS):
            at = pl.multiple_of(j * CELLS + i * 128, 128)
            rot[pl.ds(at, 128), :] = pltpu.roll(cells, 16 * j, 1) if j else cells
        return carry

    lax.fori_loop(0, CELLS // 128, turn, 0)
    stage[...] = jnp.zeros(stage.shape, jnp.float32)
    acc[...] = jnp.zeros(acc.shape, jnp.float32)

    def gather(dest):
        base = dest * CAP
        for k in range(CAP):
            u, r = k // ROWS, k % ROWS
            lanes = slice(16 * u, 16 * u + 16)
            stage[r : r + 1, lanes] = rot[pl.ds(idx_ref[base + k], 1), lanes]
        return stage[...].astype(jnp.bfloat16)

    recv[me] = gather(me)
    pl.semaphore_wait(barrier, ND - 1)

    def push(n, carry):
        t = n // PERQ
        i = lax.rem(n, PERQ)
        dest = lax.rem(mq + t, QUART) * PERQ + lax.rem(ml + i, PERQ)
        send[dest] = gather(dest)
        pltpu.make_async_remote_copy(
            src_ref=send.at[dest],
            dst_ref=recv.at[me],
            send_sem=send_sem,
            recv_sem=recv_sem.at[t],
            device_id=(dest // N_COL, lax.rem(dest, N_COL)),
            device_id_type=MESH,
        ).start()
        return carry

    lax.fori_loop(1, ND, push, 0)

    def add_up(t):
        first = lax.rem(mq - t + QUART, QUART) * PERQ
        for g in range(PERQ):
            at = pl.multiple_of((first + g) * PADR, 8)
            wide[pl.ds(at, PADR), :] = recv[first + g].astype(jnp.float32)

        def chunk(c, carry):
            at = pl.multiple_of(first * PADR + c * 128, 128)
            cols = jnp.transpose(wide[pl.ds(at, 128), :])
            masked, low = [], []
            for u in range(UNITS):
                foot = foot_ref[pl.ds(u, 1), pl.ds(at, 128)]
                hi = jnp.broadcast_to(lax.shift_right_logical(foot, 7), (BANDS, 128))
                lo = jnp.broadcast_to(foot & 127, (128, 128))
                vals = cols[16 * u : 16 * u + 16]
                masked.append(
                    jnp.concatenate([jnp.where(hi == h, vals, 0.0) for h in range(HI)], axis=0).astype(
                        jnp.bfloat16
                    )
                )
                hit = lo == lax.broadcasted_iota(jnp.int32, (128, 128), 0)
                low.append(jnp.where(hit, 1.0, 0.0).astype(jnp.bfloat16))
            acc[...] += lax.dot_general(
                jnp.concatenate(masked, axis=1),
                jnp.concatenate(low, axis=1),
                (((1,), (1,)), ((), ())),
                preferred_element_type=jnp.float32,
            )
            return carry

        lax.fori_loop(0, PERQ * PADR // 128, chunk, 0)

    for t in range(QUART):
        count = PERQ - 1 if t == 0 else PERQ
        pltpu.make_async_copy(send.at[pl.ds(0, count)], recv.at[pl.ds(0, count)], recv_sem.at[t]).wait()
        add_up(t)
    for h in range(HI):
        out_ref[:, 128 * h : 128 * h + 128] = acc[16 * h : 16 * h + 16, :] * (1.0 / NSAMP)
    pltpu.make_async_copy(send.at[pl.ds(0, ND - 1)], recv.at[pl.ds(0, ND - 1)], send_sem).wait()


def with_halo(cells, axis, dim, width):
    count = lax.axis_size(axis)
    head = lax.slice_in_dim(cells, 0, width, axis=dim)
    tail = lax.slice_in_dim(cells, cells.shape[dim] - width, cells.shape[dim], axis=dim)
    before = lax.ppermute(tail, axis, [(i, i + 1) for i in range(count - 1)])
    after = lax.ppermute(head, axis, [(i + 1, i) for i in range(count - 1)])
    return before, cells, after


def body(disk, response, spectra, srf, send_pix, recv_foot):
    margin = KS // 2
    vmem = pl.BlockSpec(memory_space=pltpu.VMEM)

    shifts = np.arange(256)[:, None] - np.arange(128)[None, :]
    picker = jnp.asarray(
        (shifts[None] == np.arange(KS)[:, None, None]).reshape(KS, -1), dtype=jnp.bfloat16
    )
    taps = jnp.pad(response, ((1, 1), (0, 0)))
    bands = jnp.dot(taps, picker, preferred_element_type=jnp.float32).astype(jnp.bfloat16)
    bands = bands.reshape(KS + 2, 256, 128)

    turned = jnp.transpose(disk, (1, 0, 2))
    rows = jnp.concatenate(with_halo(turned, "row", 0, margin), axis=0)
    cols = jnp.concatenate(with_halo(rows, "col", 2, margin), axis=2)
    padded = jnp.pad(cols, ((0, 2), (0, 0), (0, 640 - TC - 2 * margin)))
    padded = padded.reshape(74, 2, BANDS, 640)

    blurred, table = pl.pallas_call(
        blur_kernel,
        out_shape=(
            jax.ShapeDtypeStruct((BANDS, TR, TC), jnp.bfloat16),
            jax.ShapeDtypeStruct((CELLS, 128), jnp.float32),
        ),
        in_specs=[vmem, vmem],
        out_specs=(vmem, vmem),
        scratch_shapes=[pltpu.VMEM((4, 256, 128), jnp.float32)],
        compiler_params=pltpu.CompilerParams(vmem_limit_bytes=40 << 20),
        cost_estimate=pl.CostEstimate(flops=10 << 30, bytes_accessed=10 << 20, transcendentals=0),
        name="blur",
    )(padded, bands)

    slot = lax.rem(lax.iota(jnp.int32, ND * CAP), jnp.int32(CAP)) // ROWS
    cell = ((send_pix >> 12) << 9) | (send_pix & 511)
    idx = (((slot - (send_pix >> 9)) & 7) << 13) | cell

    foot = recv_foot.reshape(ND, UNITS, ROWS)
    foot = jnp.pad(foot, ((0, 0), (0, 0), (0, PADR - ROWS)), constant_values=FPD)
    foot = jnp.transpose(foot, (1, 0, 2)).reshape(UNITS, ND * PADR)

    partial_bands = jnp.dot(srf, spectra, preferred_element_type=jnp.float32)
    evolved = lax.psum_scatter(partial_bands, "col", scatter_dimension=1, tiled=True)

    imager = pl.pallas_call(
        collect_kernel,
        out_shape=jax.ShapeDtypeStruct((BANDS, FPD), jnp.float32),
        in_specs=[pl.BlockSpec(memory_space=pltpu.SMEM), vmem, vmem],
        out_specs=vmem,
        scratch_shapes=[
            pltpu.VMEM((UNITS * CELLS, 128), jnp.float32),
            pltpu.VMEM((PADR, 128), jnp.float32),
            pltpu.VMEM((ND, PADR, 128), jnp.bfloat16),
            pltpu.VMEM((ND, PADR, 128), jnp.bfloat16),
            pltpu.VMEM((ND * PADR, 128), jnp.float32),
            pltpu.VMEM((HI * BANDS, 128), jnp.float32),
            pltpu.SemaphoreType.DMA,
            pltpu.SemaphoreType.DMA((QUART,)),
        ],
        compiler_params=pltpu.CompilerParams(
            vmem_limit_bytes=52 << 20, collective_id=0, has_side_effects=True
        ),
        cost_estimate=pl.CostEstimate(flops=4 << 30, bytes_accessed=10 << 20, transcendentals=0),
        name="collect",
    )(idx, table, foot)
    return (blurred, evolved - imager)


def solution(mesh):
    placed = (
        P(None, "row", "col"),
        P(),
        P("col", "row"),
        P(None, "col"),
        P(("row", "col")),
        P(("row", "col")),
    )
    return jax.shard_map(
        body,
        mesh=mesh,
        in_specs=placed,
        out_specs=(P(None, "row", "col"), P(None, ("row", "col"))),
        check_vma=False,
    )
```

```python
import jax
import jax.numpy as jnp
from jax import lax
from jax.experimental import pallas as pl
from jax.experimental.pallas import tpu as pltpu
from jax.sharding import PartitionSpec as P

NSAMP = 16
BANDS = 16
KS = 19
EDGE = KS // 2
TR = 128
TC = 512
FPD = 1536
ND = 128
N_ROW = 32
N_COL = 4
CAP = 288
UNITS = 8
ROWS = CAP // UNITS
PADR = 40
CELLS = TR // 8 * TC
HI = FPD // 128
SLOTS = 6
TRIPS = 21
LAG = 8
MESH = pl.DeviceIdType.MESH
F32 = jnp.float32
BF16 = jnp.bfloat16


def kernel(
    turned, taps, srf_ref, spectra, idx_ref, foot_ref, blur_out, miss_out,
    own, p_ref, w_ref, spec, part, gains, edge, hrow, hcol, hcor, accb, s_ref, rot, stage, send, recv,
    acc, sm, own_sem, spec_sem, idx_sem, edge_send, edge_recv, part_send, part_recv, send_sem, recv_sem,
):
    row = lax.axis_index("row")
    col = lax.axis_index("col")
    me = row * N_COL + col

    def place(d):
        return (d // N_COL, lax.rem(d, N_COL))

    own_copy = pltpu.make_async_copy(turned, own, own_sem)
    own_copy.start()
    spec_copies = []
    for k in (1, 2, 3, 0):
        at = pl.multiple_of(lax.rem(col + k, N_COL) * FPD, 128)
        copy = pltpu.make_async_copy(spectra.at[:, pl.ds(at, FPD)], spec.at[k], spec_sem.at[k])
        copy.start()
        spec_copies.append((k, copy))

    def step_of(q):
        return q - 1

    def fetch(n, g):
        return pltpu.make_async_copy(idx_ref.at[lax.rem(me + n, ND)], sm.at[g], idx_sem.at[g])

    for g in range(SLOTS):
        fetch((0, ND - 1)[g] if g < 2 else step_of(g), g).start()

    barrier = pltpu.get_barrier_semaphore()

    def greet(i, carry):
        pl.semaphore_signal(barrier, inc=1, device_id=place(lax.rem(me + i, ND)), device_id_type=MESH)
        return carry

    lax.fori_loop(1, ND, greet, 0)

    lane = lax.broadcasted_iota(jnp.int32, (BANDS, 128), 1)
    own_copy.wait()

    def pack(g, carry):
        left = jnp.zeros((BANDS, 128), F32)
        right = jnp.zeros((BANDS, 128), F32)
        for k in range(8):
            a = own[8 * g + k, :, 0:128].astype(F32)
            b = own[8 * g + k, :, TC - 128 : TC].astype(F32)
            left = jnp.where(lane // 16 == k, pltpu.roll(a, 16 * k, 1) if k else a, left)
            right = jnp.where(lane // 16 == k, pltpu.roll(b, (16 * k + EDGE) % 128, 1), right)
        edge[0, g] = left.astype(BF16)
        edge[1, g] = right.astype(BF16)
        return carry

    lax.fori_loop(0, TR // 8, pack, 0)
    pl.semaphore_wait(barrier, ND - 1)

    up, down = lax.rem(row + N_ROW - 1, N_ROW), lax.rem(row + 1, N_ROW)
    west, east = lax.rem(col + N_COL - 1, N_COL), lax.rem(col + 1, N_COL)
    moves = [
        (own.at[pl.ds(0, EDGE)], hrow.at[1], (up, col)),
        (own.at[pl.ds(TR - EDGE, EDGE)], hrow.at[0], (down, col)),
        (edge.at[0], hcol.at[1], (row, west)),
        (edge.at[1], hcol.at[0], (row, east)),
        (edge.at[0, pl.ds(0, 2)], hcor.at[3], (up, west)),
        (edge.at[1, pl.ds(0, 2)], hcor.at[2], (up, east)),
        (edge.at[0, pl.ds(14, 2)], hcor.at[1], (down, west)),
        (edge.at[1, pl.ds(14, 2)], hcor.at[0], (down, east)),
    ]
    edge_copies = [
        pltpu.make_async_remote_copy(
            src_ref=src, dst_ref=dst, send_sem=edge_send.at[i], recv_sem=edge_recv.at[i],
            device_id=there, device_id_type=MESH,
        )
        for i, (src, dst, there) in enumerate(moves)
    ]
    for copy in edge_copies:
        copy.start()

    part_copies = []
    for k, copy in spec_copies:
        copy.wait()
        part[k] = jnp.dot(srf_ref[...], spec[k], preferred_element_type=F32)
        if k:
            out = pltpu.make_async_remote_copy(
                src_ref=part.at[k], dst_ref=gains.at[k], send_sem=part_send.at[k], recv_sem=part_recv.at[k],
                device_id=(row, lax.rem(col + k, N_COL)), device_id_type=MESH,
            )
            out.start()
            part_copies.append(out)

    w_ref[0] = jnp.zeros((256, 128), BF16)
    w_ref[KS + 1] = jnp.zeros((256, 128), BF16)

    def band(a, carry):
        line = jnp.broadcast_to(taps[pl.ds(a, 1), :], (256, 256))
        w_ref[a + 1] = pltpu.roll(line, 0, 1, stride=1, stride_axis=0)[:, :128].astype(BF16)
        return carry

    lax.fori_loop(0, KS, band, 0)

    blank = jnp.zeros((BANDS, 128), F32)

    def shifted(cells):
        return pltpu.roll(jnp.concatenate([cells.astype(F32), blank], axis=1), EDGE, 1)

    def lay(g, carry):
        for k in range(8):
            y = k + EDGE
            p_ref[4 * g + y // 2, y % 2] = shifted(own[8 * g + k]).astype(BF16)
        return carry

    lax.fori_loop(0, TR // 8, lay, 0)
    p_ref[73, 0] = jnp.zeros((BANDS, 640), BF16)
    p_ref[73, 1] = jnp.zeros((BANDS, 640), BF16)

    for copy in edge_copies:
        copy.wait_recv()

    has_up, has_down = row > 0, row < N_ROW - 1
    has_west, has_east = col > 0, col < N_COL - 1

    def west_side(packed, k, tile, keep):
        piece = packed.astype(F32)
        piece = pltpu.roll(piece, 128 - 16 * k, 1) if k else piece
        return jnp.where(lane < EDGE, jnp.where(keep, piece, 0.0), tile)

    def east_side(packed, k, tile, keep):
        piece = pltpu.roll(packed.astype(F32), (128 + EDGE - 16 * k) % 128, 1)
        return jnp.where((lane >= EDGE) & (lane < 2 * EDGE), jnp.where(keep, piece, 0.0), tile)

    def sides(g, carry):
        for k in range(8):
            y = k + EDGE
            at = (4 * g + y // 2, y % 2)
            p_ref[at[0], at[1], :, 0:128] = west_side(
                hcol[0, g], k, p_ref[at[0], at[1], :, 0:128].astype(F32), has_west
            ).astype(BF16)
            p_ref[at[0], at[1], :, TC : TC + 128] = east_side(
                hcol[1, g], k, p_ref[at[0], at[1], :, TC : TC + 128].astype(F32), has_east
            ).astype(BF16)
        return carry

    lax.fori_loop(0, TR // 8, sides, 0)
    for half, first, keep in ((0, 8 - 1, has_up), (1, 0, has_down)):
        for i in range(EDGE):
            y = i if half == 0 else TR + EDGE + i
            g, k = (first + i) // 8, (first + i) % 8
            line = shifted(jnp.where(keep, hrow[half, i].astype(F32), 0.0))
            west_tile = west_side(hcor[2 * half, g], k, line[:, :128], keep & has_west)
            east_tile = east_side(hcor[2 * half + 1, g], k, line[:, TC:], keep & has_east)
            whole = jnp.concatenate([west_tile, line[:, 128:TC], east_tile], axis=1)
            p_ref[y // 2, y % 2] = whole.astype(BF16)

    def products(yb):
        total = None
        for a in range(KS + 1):
            left = jnp.concatenate(
                [
                    p_ref[pl.ds(yb * 8 + a // 2, 8), a % 2, :, j * 128 : j * 128 + 256].reshape(128, 256)
                    for j in range(4)
                ],
                axis=0,
            )
            right = jnp.concatenate([w_ref[a + 1], w_ref[a]], axis=1)
            term = jnp.dot(left, right, preferred_element_type=F32)
            total = term if total is None else total + term
        return total

    def settle(yb):
        rounded = accb[...].astype(BF16).astype(F32)
        for j in range(4):
            lines = [
                rounded[j * 128 + m * 16 : j * 128 + m * 16 + 16, q * 128 : q * 128 + 128]
                for m in range(8)
                for q in range(2)
            ]
            for h in range(2):
                piece = jnp.concatenate(lines[8 * h : 8 * h + 8], axis=0)
                s_ref[j, pl.ds(h * 128, 128), :] = piece
                cells = jnp.transpose(piece)
                for t in range(UNITS):
                    at = pl.multiple_of(t * CELLS + (2 * yb + h) * TC + j * 128, 128)
                    rot[pl.ds(at, 128), :] = pltpu.roll(cells, 16 * t, 1) if t else cells
            for b in range(BANDS):
                blur_out[b, pl.ds(pl.multiple_of(yb * 16, 16), 16), j * 128 : j * 128 + 128] = s_ref[
                    j, pl.ds(b, 16, stride=16), :
                ].astype(BF16)

    accb[...] = products(0)

    def block(yb, carry):
        settle(yb - 1)
        accb[...] = products(yb)
        return carry

    lax.fori_loop(1, TR // 16, block, 0)
    settle(TR // 16 - 1)

    stage[...] = jnp.zeros(stage.shape, F32)
    acc[...] = jnp.zeros(acc.shape, F32)
    lane8 = lax.broadcasted_iota(jnp.int32, (UNITS, 128), 1)

    def gather(g):
        for k in range(CAP):
            u, r = k // ROWS, k % ROWS
            lanes = slice(16 * u, 16 * u + 16)
            stage[g, r : r + 1, lanes] = rot[pl.ds(sm[g, 0, k], 1), lanes]
        return stage[g].astype(BF16)

    def message(n, mark):
        return pltpu.make_async_remote_copy(
            src_ref=send.at[n], dst_ref=recv.at[n], send_sem=send_sem, recv_sem=recv_sem.at[mark],
            device_id=place(lax.rem(me + n, ND)), device_id_type=MESH,
        )

    def arrived(n, count, mark):
        pltpu.make_async_copy(send.at[pl.ds(n, count)], recv.at[pl.ds(n, count)], recv_sem.at[mark]).wait()

    def add_up(steps):
        blocks = [recv[n].astype(F32) for n in steps]
        blocks.append(jnp.zeros((128 - PADR * len(steps), 128), F32))
        foot = jnp.full((UNITS, 128), FPD, jnp.int32)
        for g, n in enumerate(steps):
            feet = foot_ref[lax.rem(me + ND - n, ND)]
            inside = (lane8 >= PADR * g) & (lane8 < PADR * g + PADR)
            foot = jnp.where(inside, pltpu.roll(feet, PADR * g, 1) if g else feet, foot)
        cols = jnp.transpose(jnp.concatenate(blocks, axis=0))
        masked, low = [], []
        for u in range(UNITS):
            hi = jnp.broadcast_to(lax.shift_right_logical(foot[u : u + 1], 7), (BANDS, 128))
            lo = jnp.broadcast_to(foot[u : u + 1] & 127, (128, 128))
            vals = cols[16 * u : 16 * u + 16]
            masked.append(
                jnp.concatenate([jnp.where(hi == h, vals, 0.0) for h in range(HI)], axis=0).astype(BF16)
            )
            hit = lo == lax.broadcasted_iota(jnp.int32, (128, 128), 0)
            low.append(jnp.where(hit, 1.0, 0.0).astype(BF16))
        acc[...] += lax.dot_general(
            jnp.concatenate(masked, axis=1),
            jnp.concatenate(low, axis=1),
            (((1,), (1,)), ((), ())),
            preferred_element_type=F32,
        )

    for g, n in ((0, 0), (1, ND - 1)):
        fetch(n, g).wait()
        if n:
            send[n] = gather(g)
            message(n, 2 * TRIPS).start()
        else:
            recv[0] = gather(g)
        fetch(step_of(g + SLOTS), g).start()

    def half(n, groups, trio, summing):
        for k, g in enumerate(groups):
            fetch(n + k, g).wait()
        if summing:
            back = n - 3 * LAG
            arrived(back, 3, trio - LAG)
            add_up([back, back + 1, back + 2])
        for k, g in enumerate(groups):
            send[n + k] = gather(g)
        for k, g in enumerate(groups):
            message(n + k, trio).start()
            fetch(jnp.minimum(n + k + SLOTS, ND - 1), g).start()

    def turns(summing):
        def turn(i, carry):
            n = 1 + 6 * i
            half(n, (2, 3, 4), 2 * i, summing)
            half(n + 3, (5, 0, 1), 2 * i + 1, summing)
            return carry

        return turn

    lax.fori_loop(0, LAG // 2, turns(False), 0)
    lax.fori_loop(LAG // 2, TRIPS, turns(True), 0)

    def rest(i, carry):
        n = 1 + 6 * i
        arrived(n, 3, 2 * i)
        arrived(n + 3, 3, 2 * i + 1)
        add_up([n, n + 1, n + 2])
        add_up([n + 3, n + 4, n + 5])
        return carry

    lax.fori_loop(TRIPS - LAG // 2, TRIPS, rest, 0)
    arrived(ND - 1, 1, 2 * TRIPS)
    add_up([0, ND - 1])

    for copy in part_copies:
        copy.wait_recv()
    for h in range(HI):
        lanes = slice(128 * h, 128 * h + 128)
        evolved = part[0, :, lanes]
        for k in range(1, N_COL):
            evolved = evolved + gains[k, :, lanes]
        miss_out[:, lanes] = evolved - acc[16 * h : 16 * h + 16, :] * (1.0 / NSAMP)

    for g in range(SLOTS):
        fetch(0, g).wait()
    for copy in edge_copies + part_copies:
        copy.wait_send()
    pltpu.make_async_copy(send.at[pl.ds(1, ND - 1)], recv.at[pl.ds(1, ND - 1)], send_sem).wait()


def body(disk, response, spectra, srf, send_pix, recv_foot):
    vmem = pl.BlockSpec(memory_space=pltpu.VMEM)
    hbm = pl.BlockSpec(memory_space=pl.ANY)

    turned = jnp.transpose(disk, (1, 0, 2))
    wide = response.astype(F32)
    taps = jnp.concatenate([wide[:, :1], jnp.zeros((KS, 256 - KS), F32), wide[:, :0:-1]], axis=1)

    slot = lax.rem(lax.iota(jnp.int32, ND * CAP), jnp.int32(CAP)) // ROWS
    cell = ((send_pix >> 12) << 9) | (send_pix & 511)
    idx = (((slot - (send_pix >> 9)) & 7) << 13) | cell
    idx = jnp.pad(idx.reshape(ND, 1, CAP), ((0, 0), (0, 0), (0, 384 - CAP)))

    foot = recv_foot.reshape(ND, UNITS, ROWS)
    foot = jnp.pad(foot, ((0, 0), (0, 0), (0, 128 - ROWS)), constant_values=FPD)

    dma = pltpu.SemaphoreType.DMA
    return tuple(
        pl.pallas_call(
            kernel,
            out_shape=(
                jax.ShapeDtypeStruct((BANDS, TR, TC), BF16),
                jax.ShapeDtypeStruct((BANDS, FPD), F32),
            ),
            in_specs=[hbm, vmem, vmem, hbm, hbm, vmem],
            out_specs=(vmem, vmem),
            scratch_shapes=[
                pltpu.VMEM((TR, BANDS, TC), BF16),
                pltpu.VMEM((74, 2, BANDS, 640), BF16),
                pltpu.VMEM((KS + 2, 256, 128), BF16),
                pltpu.VMEM((N_COL, 512, FPD), BF16),
                pltpu.VMEM((N_COL, BANDS, FPD), F32),
                pltpu.VMEM((N_COL, BANDS, FPD), F32),
                pltpu.VMEM((2, 16, BANDS, 128), BF16),
                pltpu.VMEM((2, EDGE, BANDS, TC), BF16),
                pltpu.VMEM((2, 16, BANDS, 128), BF16),
                pltpu.VMEM((4, 2, BANDS, 128), BF16),
                pltpu.VMEM((512, 256), F32),
                pltpu.VMEM((4, 256, 128), F32),
                pltpu.VMEM((UNITS * CELLS, 128), F32),
                pltpu.VMEM((SLOTS, PADR, 128), F32),
                pltpu.VMEM((ND, PADR, 128), BF16),
                pltpu.VMEM((ND, PADR, 128), BF16),
                pltpu.VMEM((HI * BANDS, 128), F32),
                pltpu.SMEM((SLOTS, 1, 384), jnp.int32),
                dma,
                dma((N_COL,)),
                dma((SLOTS,)),
                dma((8,)),
                dma((8,)),
                dma((N_COL,)),
                dma((N_COL,)),
                dma,
                dma((2 * TRIPS + 1,)),
            ],
            compiler_params=pltpu.CompilerParams(
                vmem_limit_bytes=60 << 20, collective_id=0, has_side_effects=True
            ),
            cost_estimate=pl.CostEstimate(flops=16 << 30, bytes_accessed=16 << 20, transcendentals=0),
            name="collocate",
        )(turned, taps, srf, spectra, idx, foot)
    )


def solution(mesh):
    placed = (
        P(None, "row", "col"),
        P(),
        P("col", "row"),
        P(None, "col"),
        P(("row", "col")),
        P(("row", "col")),
    )
    return jax.shard_map(
        body,
        mesh=mesh,
        in_specs=placed,
        out_specs=(P(None, "row", "col"), P(None, ("row", "col"))),
        check_vma=False,
    )
```

```python
import jax
import jax.numpy as jnp
from jax import lax
from jax.experimental import pallas as pl
from jax.experimental.pallas import tpu as pltpu
from jax.sharding import PartitionSpec as P

NSAMP = 16
BANDS = 16
KS = 19
EDGE = KS // 2
TR = 128
TC = 512
FPD = 1536
ND = 128
N_ROW = 32
N_COL = 4
CAP = 288
UNITS = 8
ROWS = CAP // UNITS
PADR = 40
CELLS = TR // 8 * TC
HI = FPD // 128
BATCH = 3
SLOTS = 2 * BATCH
TRIPS = 21
LAG = 12
TRIOS = 2 * TRIPS
MESH = pl.DeviceIdType.MESH
F32 = jnp.float32
BF16 = jnp.bfloat16


def kernel(
    turned, taps, srf_ref, spectra, idx_ref, foot_ref, blur_out, miss_out,
    own, p_ref, w_ref, lines, spec, part, gains, edge, hrow, hcol, hcor, accb, s_ref, rot, stage, send, recv,
    acc, sm, ring, own_sem, spec_sem, idx_sem, edge_send, edge_recv, part_send, part_recv, send_sem, recv_sem,
):
    row = lax.axis_index("row")
    col = lax.axis_index("col")
    me = row * N_COL + col

    def place(d):
        r = lax.div(d, N_COL)
        return (r, d - r * N_COL)

    own_copy = pltpu.make_async_copy(turned, own, own_sem)
    own_copy.start()
    spec_copies = []
    for k in (1, 2, 3, 0):
        at = pl.multiple_of(lax.rem(col + k, N_COL) * FPD, 128)
        copy = pltpu.make_async_copy(spectra.at[:, pl.ds(at, FPD)], spec.at[k], spec_sem.at[k])
        copy.start()
        spec_copies.append((k, copy))

    def step_of(q):
        return q - 1

    def fetch(n, g):
        return pltpu.make_async_copy(idx_ref.at[lax.rem(me + n, ND)], sm.at[g], idx_sem.at[g])

    for g in range(SLOTS):
        fetch((0, ND - 1)[g] if g < 2 else step_of(g), g).start()

    def around(value, by, count):
        moved = value + by
        return jnp.where(moved >= count, moved - count, jnp.where(moved < 0, moved + count, moved))

    barrier = pltpu.get_barrier_semaphore()
    for dr, dc in [(0, 1), (0, 2), (0, 3)] + [(dr, dc) for dr in (1, -1) for dc in range(N_COL)]:
        there = (around(row, dr, N_ROW), around(col, dc, N_COL))
        pl.semaphore_signal(barrier, inc=1, device_id=there, device_id_type=MESH)

    def ring_tell(level):
        for by in (1 << level, -(1 << level)):
            pl.semaphore_signal(
                ring.at[level], inc=1, device_id=(around(row, by, N_ROW), col), device_id_type=MESH
            )

    def ring_hear(level):
        pl.semaphore_wait(ring.at[level], 2)

    lane = lax.broadcasted_iota(jnp.int32, (BANDS, 128), 1)
    own_copy.wait()

    def pack(g, carry):
        left = jnp.zeros((BANDS, 128), F32)
        right = jnp.zeros((BANDS, 128), F32)
        for k in range(8):
            a = own[8 * g + k, :, 0:128].astype(F32)
            b = own[8 * g + k, :, TC - 128 : TC].astype(F32)
            left = jnp.where(lane // 16 == k, pltpu.roll(a, 16 * k, 1) if k else a, left)
            right = jnp.where(lane // 16 == k, pltpu.roll(b, (16 * k + EDGE) % 128, 1), right)
        edge[0, g] = left.astype(BF16)
        edge[1, g] = right.astype(BF16)
        return carry

    lax.fori_loop(0, TR // 8, pack, 0)
    pl.semaphore_wait(barrier, 2 * N_COL + N_COL - 1)

    up, down = lax.rem(row + N_ROW - 1, N_ROW), lax.rem(row + 1, N_ROW)
    west, east = lax.rem(col + N_COL - 1, N_COL), lax.rem(col + 1, N_COL)
    moves = [
        (own.at[pl.ds(0, EDGE)], hrow.at[1], (up, col)),
        (own.at[pl.ds(TR - EDGE, EDGE)], hrow.at[0], (down, col)),
        (edge.at[0], hcol.at[1], (row, west)),
        (edge.at[1], hcol.at[0], (row, east)),
        (edge.at[0, pl.ds(0, 2)], hcor.at[3], (up, west)),
        (edge.at[1, pl.ds(0, 2)], hcor.at[2], (up, east)),
        (edge.at[0, pl.ds(14, 2)], hcor.at[1], (down, west)),
        (edge.at[1, pl.ds(14, 2)], hcor.at[0], (down, east)),
    ]
    edge_copies = [
        pltpu.make_async_remote_copy(
            src_ref=src, dst_ref=dst, send_sem=edge_send.at[i], recv_sem=edge_recv.at[i],
            device_id=there, device_id_type=MESH,
        )
        for i, (src, dst, there) in enumerate(moves)
    ]
    for copy in edge_copies:
        copy.start()
    ring_tell(0)

    part_copies = []
    for k, copy in spec_copies:
        copy.wait()
        part[k] = jnp.dot(srf_ref[...], spec[k], preferred_element_type=F32)
        if k:
            out = pltpu.make_async_remote_copy(
                src_ref=part.at[k], dst_ref=gains.at[k], send_sem=part_send.at[k], recv_sem=part_recv.at[k],
                device_id=(row, lax.rem(col + k, N_COL)), device_id_type=MESH,
            )
            out.start()
            part_copies.append(out)

    w_ref[0] = jnp.zeros((256, 128), BF16)
    w_ref[KS + 1] = jnp.zeros((256, 128), BF16)

    tap = lax.broadcasted_iota(jnp.int32, (128, 256), 0)
    at = lax.broadcasted_iota(jnp.int32, (128, 256), 1)
    flip = jnp.where((tap + at == 256) | ((tap == 0) & (at == 0)), 1.0, 0.0).astype(BF16)
    lines[...] = jnp.dot(taps[...], flip, preferred_element_type=F32)

    def band(a, carry):
        line = jnp.broadcast_to(lines[pl.ds(a, 1), :], (256, 256))
        w_ref[a + 1] = pltpu.roll(line, 0, 1, stride=1, stride_axis=0)[:, :128].astype(BF16)
        return carry

    lax.fori_loop(0, KS, band, 0)

    blank = jnp.zeros((BANDS, 128), F32)

    def shifted(cells):
        return pltpu.roll(jnp.concatenate([cells.astype(F32), blank], axis=1), EDGE, 1)

    def lay(g, carry):
        for k in range(8):
            y = k + EDGE
            p_ref[4 * g + y // 2, y % 2] = shifted(own[8 * g + k]).astype(BF16)
        return carry

    lax.fori_loop(0, TR // 8, lay, 0)
    p_ref[73, 0] = jnp.zeros((BANDS, 640), BF16)
    p_ref[73, 1] = jnp.zeros((BANDS, 640), BF16)

    for copy in edge_copies:
        copy.wait_recv()
    ring_hear(0)
    ring_tell(1)

    has_up, has_down = row > 0, row < N_ROW - 1
    has_west, has_east = col > 0, col < N_COL - 1

    def west_side(packed, k, tile, keep):
        piece = packed.astype(F32)
        piece = pltpu.roll(piece, 128 - 16 * k, 1) if k else piece
        return jnp.where(lane < EDGE, jnp.where(keep, piece, 0.0), tile)

    def east_side(packed, k, tile, keep):
        piece = pltpu.roll(packed.astype(F32), (128 + EDGE - 16 * k) % 128, 1)
        return jnp.where((lane >= EDGE) & (lane < 2 * EDGE), jnp.where(keep, piece, 0.0), tile)

    def sides(g, carry):
        for k in range(8):
            y = k + EDGE
            at = (4 * g + y // 2, y % 2)
            p_ref[at[0], at[1], :, 0:128] = west_side(
                hcol[0, g], k, p_ref[at[0], at[1], :, 0:128].astype(F32), has_west
            ).astype(BF16)
            p_ref[at[0], at[1], :, TC : TC + 128] = east_side(
                hcol[1, g], k, p_ref[at[0], at[1], :, TC : TC + 128].astype(F32), has_east
            ).astype(BF16)
        return carry

    lax.fori_loop(0, TR // 8, sides, 0)
    for half, first, keep in ((0, 8 - 1, has_up), (1, 0, has_down)):
        for i in range(EDGE):
            y = i if half == 0 else TR + EDGE + i
            g, k = (first + i) // 8, (first + i) % 8
            line = shifted(jnp.where(keep, hrow[half, i].astype(F32), 0.0))
            west_tile = west_side(hcor[2 * half, g], k, line[:, :128], keep & has_west)
            east_tile = east_side(hcor[2 * half + 1, g], k, line[:, TC:], keep & has_east)
            whole = jnp.concatenate([west_tile, line[:, 128:TC], east_tile], axis=1)
            p_ref[y // 2, y % 2] = whole.astype(BF16)

    def products(yb):
        total = None
        for a in range(KS + 1):
            left = jnp.concatenate(
                [
                    p_ref[pl.ds(yb * 8 + a // 2, 8), a % 2, :, j * 128 : j * 128 + 256].reshape(128, 256)
                    for j in range(4)
                ],
                axis=0,
            )
            right = jnp.concatenate([w_ref[a + 1], w_ref[a]], axis=1)
            term = jnp.dot(left, right, preferred_element_type=F32)
            total = term if total is None else total + term
        return total

    def settle(yb):
        rounded = accb[...].astype(BF16).astype(F32)
        for j in range(4):
            strips = [
                rounded[j * 128 + m * 16 : j * 128 + m * 16 + 16, q * 128 : q * 128 + 128]
                for m in range(8)
                for q in range(2)
            ]
            for h in range(2):
                piece = jnp.concatenate(strips[8 * h : 8 * h + 8], axis=0)
                s_ref[j, pl.ds(h * 128, 128), :] = piece
                cells = jnp.transpose(piece)
                for t in range(UNITS):
                    at = pl.multiple_of(t * CELLS + (2 * yb + h) * TC + j * 128, 128)
                    rot[pl.ds(at, 128), :] = pltpu.roll(cells, 16 * t, 1) if t else cells
            for b in range(BANDS):
                blur_out[b, pl.ds(pl.multiple_of(yb * 16, 16), 16), j * 128 : j * 128 + 128] = s_ref[
                    j, pl.ds(b, 16, stride=16), :
                ].astype(BF16)

    accb[...] = products(0)
    ring_hear(1)
    ring_tell(2)

    def block(yb, carry):
        settle(yb - 1)
        accb[...] = products(yb)
        return carry

    lax.fori_loop(1, 3, block, 0)
    ring_hear(2)
    ring_tell(3)
    lax.fori_loop(3, TR // 16, block, 0)
    ring_hear(3)
    settle(TR // 16 - 1)

    stage[...] = jnp.zeros(stage.shape, F32)
    acc[...] = jnp.zeros(acc.shape, F32)
    lane8 = lax.broadcasted_iota(jnp.int32, (UNITS, 128), 1)

    def gather(g):
        for k in range(CAP):
            u, r = k // ROWS, k % ROWS
            lanes = slice(16 * u, 16 * u + 16)
            stage[g, r : r + 1, lanes] = rot[pl.ds(sm[g, 0, k], 1), lanes]
        return stage[g].astype(BF16)

    def message(n, mark):
        return pltpu.make_async_remote_copy(
            src_ref=send.at[n], dst_ref=recv.at[n], send_sem=send_sem, recv_sem=recv_sem.at[mark],
            device_id=place(lax.rem(me + n, ND)), device_id_type=MESH,
        )

    def arrived(n, count, mark):
        pltpu.make_async_copy(send.at[pl.ds(n, count)], recv.at[pl.ds(n, count)], recv_sem.at[mark]).wait()

    def add_up(steps):
        blocks = [recv[n].astype(F32) for n in steps]
        blocks.append(jnp.zeros((128 - PADR * len(steps), 128), F32))
        foot = jnp.full((UNITS, 128), FPD, jnp.int32)
        for g, n in enumerate(steps):
            feet = foot_ref[lax.rem(me + ND - n, ND)]
            inside = (lane8 >= PADR * g) & (lane8 < PADR * g + PADR)
            foot = jnp.where(inside, pltpu.roll(feet, PADR * g, 1) if g else feet, foot)
        cols = jnp.transpose(jnp.concatenate(blocks, axis=0))
        masked, low = [], []
        for u in range(UNITS):
            hi = jnp.broadcast_to(lax.shift_right_logical(foot[u : u + 1], 7), (BANDS, 128))
            lo = jnp.broadcast_to(foot[u : u + 1] & 127, (128, 128))
            vals = cols[16 * u : 16 * u + 16]
            masked.append(
                jnp.concatenate([jnp.where(hi == h, vals, 0.0) for h in range(HI)], axis=0).astype(BF16)
            )
            hit = lo == lax.broadcasted_iota(jnp.int32, (128, 128), 0)
            low.append(jnp.where(hit, 1.0, 0.0).astype(BF16))
        acc[...] += lax.dot_general(
            jnp.concatenate(masked, axis=1),
            jnp.concatenate(low, axis=1),
            (((1,), (1,)), ((), ())),
            preferred_element_type=F32,
        )

    for g, n in ((0, 0), (1, ND - 1)):
        fetch(n, g).wait()
        if n:
            send[n] = gather(g)
            message(n, TRIOS).start()
        else:
            recv[0] = gather(g)
        fetch(step_of(g + SLOTS), g).start()

    def sums(first, waiting):
        trio = lax.div(first, 3)
        if waiting:
            arrived(first, 3, trio)
        add_up([first, first + 1, first + 2])

    def segment(n, slots, summing):
        trio = lax.div(n, 3)
        for k, g in enumerate(slots):
            fetch(n + k, g).wait()
        if summing:
            sums(n - BATCH * LAG, True)
        for k, g in enumerate(slots):
            send[n + k] = gather(g)
        for k, g in enumerate(slots):
            fetch(jnp.minimum(n + k + SLOTS, ND - 1), g).start()
        for k in range(BATCH):
            message(n + k, trio).start()

    early = tuple(range(2, 2 + BATCH))
    late = tuple((2 + BATCH + k) % SLOTS for k in range(BATCH))

    def turns(summing):
        def turn(i, carry):
            n = 1 + 2 * BATCH * i
            segment(n, early, summing)
            segment(n + BATCH, late, summing)
            return carry

        return turn

    lax.fori_loop(0, LAG // 2, turns(False), 0)
    lax.fori_loop(LAG // 2, TRIPS, turns(True), 0)

    def rest(i, carry):
        sums(1 + BATCH * i, True)
        return carry

    lax.fori_loop(2 * TRIPS - LAG, 2 * TRIPS, rest, 0)
    arrived(ND - 1, 1, TRIOS)
    add_up([0, ND - 1])

    for copy in part_copies:
        copy.wait_recv()
    for h in range(HI):
        lanes = slice(128 * h, 128 * h + 128)
        evolved = part[0, :, lanes]
        for k in range(1, N_COL):
            evolved = evolved + gains[k, :, lanes]
        miss_out[:, lanes] = evolved - acc[16 * h : 16 * h + 16, :] * (1.0 / NSAMP)

    for g in range(SLOTS):
        fetch(0, g).wait()
    for copy in edge_copies + part_copies:
        copy.wait_send()
    pltpu.make_async_copy(send.at[pl.ds(1, ND - 1)], recv.at[pl.ds(1, ND - 1)], send_sem).wait()


def body(disk, response, spectra, srf, send_pix, recv_foot):
    vmem = pl.BlockSpec(memory_space=pltpu.VMEM)
    hbm = pl.BlockSpec(memory_space=pl.ANY)

    turned = jnp.transpose(disk, (1, 0, 2))
    taps = jnp.pad(response, ((0, 24 - KS), (0, 128 - KS)))

    pix = jnp.pad(send_pix.reshape(ND, 1, CAP), ((0, 0), (0, 0), (0, 384 - CAP)))
    slot = lax.broadcasted_iota(jnp.int32, pix.shape, 2) // ROWS
    idx = (((slot - (pix >> 9)) & 7) << 13) | ((pix >> 12) << 9) | (pix & 511)

    foot = recv_foot.reshape(ND, UNITS, ROWS)
    foot = jnp.pad(foot, ((0, 0), (0, 0), (0, 128 - ROWS)), constant_values=FPD)

    dma = pltpu.SemaphoreType.DMA
    return tuple(
        pl.pallas_call(
            kernel,
            out_shape=(
                jax.ShapeDtypeStruct((BANDS, TR, TC), BF16),
                jax.ShapeDtypeStruct((BANDS, FPD), F32),
            ),
            in_specs=[hbm, vmem, vmem, hbm, hbm, vmem],
            out_specs=(vmem, vmem),
            scratch_shapes=[
                pltpu.VMEM((TR, BANDS, TC), BF16),
                pltpu.VMEM((74, 2, BANDS, 640), BF16),
                pltpu.VMEM((KS + 2, 256, 128), BF16),
                pltpu.VMEM((24, 256), F32),
                pltpu.VMEM((N_COL, 512, FPD), BF16),
                pltpu.VMEM((N_COL, BANDS, FPD), F32),
                pltpu.VMEM((N_COL, BANDS, FPD), F32),
                pltpu.VMEM((2, 16, BANDS, 128), BF16),
                pltpu.VMEM((2, EDGE, BANDS, TC), BF16),
                pltpu.VMEM((2, 16, BANDS, 128), BF16),
                pltpu.VMEM((4, 2, BANDS, 128), BF16),
                pltpu.VMEM((512, 256), F32),
                pltpu.VMEM((4, 256, 128), F32),
                pltpu.VMEM((UNITS * CELLS, 128), F32),
                pltpu.VMEM((SLOTS, PADR, 128), F32),
                pltpu.VMEM((ND, PADR, 128), BF16),
                pltpu.VMEM((ND, PADR, 128), BF16),
                pltpu.VMEM((HI * BANDS, 128), F32),
                pltpu.SMEM((SLOTS, 1, 384), jnp.int32),
                pltpu.SemaphoreType.REGULAR((4,)),
                dma,
                dma((N_COL,)),
                dma((SLOTS,)),
                dma((8,)),
                dma((8,)),
                dma((N_COL,)),
                dma((N_COL,)),
                dma,
                dma((TRIOS + 1,)),
            ],
            compiler_params=pltpu.CompilerParams(
                vmem_limit_bytes=60 << 20, collective_id=0, has_side_effects=True
            ),
            cost_estimate=pl.CostEstimate(flops=16 << 30, bytes_accessed=16 << 20, transcendentals=0),
            name="collocate",
        )(turned, taps, srf, spectra, idx, foot)
    )


def solution(mesh):
    placed = (
        P(None, "row", "col"),
        P(),
        P("col", "row"),
        P(None, "col"),
        P(("row", "col")),
        P(("row", "col")),
    )
    return jax.shard_map(
        body,
        mesh=mesh,
        in_specs=placed,
        out_specs=(P(None, "row", "col"), P(None, ("row", "col"))),
        check_vma=False,
    )
```

```python
import jax
import jax.numpy as jnp
from jax import lax
from jax.experimental import pallas as pl
from jax.experimental.pallas import tpu as pltpu
from jax.sharding import PartitionSpec as P

NSAMP = 16
BANDS = 16
KS = 19
EDGE = KS // 2
TR = 128
TC = 512
FPD = 1536
ND = 128
N_ROW = 32
N_COL = 4
CAP = 288
UNITS = 8
ROWS = CAP // UNITS
PADR = 40
CELLS = TR // 8 * TC
HI = FPD // 128
BATCH = 6
SLOTS = 2 * BATCH
TRIPS = 10
LAG = 8
TRIOS = 2 * (2 * TRIPS + 1)
MESH = pl.DeviceIdType.MESH
F32 = jnp.float32
BF16 = jnp.bfloat16


def kernel(
    turned, taps, srf_ref, spectra, idx_ref, feet, blur_out, miss_out,
    own, p_ref, w_ref, lines, spec, part, gains, edge, hrow, hcol, hcor, accb, foot_ref, rot, stage, send, recv,
    acc, sm, ring, own_sem, out_sem, foot_sem, spec_sem, idx_sem, edge_send, edge_recv, part_send, part_recv, send_sem, recv_sem,
):
    row = lax.axis_index("row")
    col = lax.axis_index("col")
    me = row * N_COL + col

    def place(d):
        r = lax.div(d, N_COL)
        return (r, d - r * N_COL)

    own_copy = pltpu.make_async_copy(turned, own, own_sem)
    own_copy.start()
    foot_copy = pltpu.make_async_copy(feet, foot_ref, foot_sem)
    foot_copy.start()
    spec_copies = []
    for k in (1, 2, 3, 0):
        at = pl.multiple_of(lax.rem(col + k, N_COL) * FPD, 128)
        copy = pltpu.make_async_copy(spectra.at[:, pl.ds(at, FPD)], spec.at[k], spec_sem.at[k])
        copy.start()
        spec_copies.append((k, copy))

    def step_of(q):
        return q - 1

    def fetch(n, g):
        return pltpu.make_async_copy(idx_ref.at[lax.rem(me + n, ND)], sm.at[g], idx_sem.at[g])

    for g in range(SLOTS):
        fetch((0, ND - 1)[g] if g < 2 else step_of(g), g).start()

    def around(value, by, count):
        moved = value + by
        return jnp.where(moved >= count, moved - count, jnp.where(moved < 0, moved + count, moved))

    barrier = pltpu.get_barrier_semaphore()
    for dr, dc in [(0, 1), (0, 2), (0, 3)] + [(dr, dc) for dr in (1, -1) for dc in range(N_COL)]:
        there = (around(row, dr, N_ROW), around(col, dc, N_COL))
        pl.semaphore_signal(barrier, inc=1, device_id=there, device_id_type=MESH)

    def ring_tell(level):
        for by in (1 << level, -(1 << level)):
            pl.semaphore_signal(
                ring.at[level], inc=1, device_id=(around(row, by, N_ROW), col), device_id_type=MESH
            )

    def ring_hear(level):
        pl.semaphore_wait(ring.at[level], 2)

    lane = lax.broadcasted_iota(jnp.int32, (BANDS, 128), 1)
    own_copy.wait()

    def pack(g, carry):
        left = jnp.zeros((BANDS, 128), F32)
        right = jnp.zeros((BANDS, 128), F32)
        for k in range(8):
            a = own[8 * g + k, :, 0:128].astype(F32)
            b = own[8 * g + k, :, TC - 128 : TC].astype(F32)
            left = jnp.where(lane // 16 == k, pltpu.roll(a, 16 * k, 1) if k else a, left)
            right = jnp.where(lane // 16 == k, pltpu.roll(b, (16 * k + EDGE) % 128, 1), right)
        edge[0, g] = left.astype(BF16)
        edge[1, g] = right.astype(BF16)
        return carry

    lax.fori_loop(0, TR // 8, pack, 0)
    pl.semaphore_wait(barrier, 2 * N_COL + N_COL - 1)

    up, down = lax.rem(row + N_ROW - 1, N_ROW), lax.rem(row + 1, N_ROW)
    west, east = lax.rem(col + N_COL - 1, N_COL), lax.rem(col + 1, N_COL)
    moves = [
        (own.at[pl.ds(0, EDGE)], hrow.at[1], (up, col)),
        (own.at[pl.ds(TR - EDGE, EDGE)], hrow.at[0], (down, col)),
        (edge.at[0], hcol.at[1], (row, west)),
        (edge.at[1], hcol.at[0], (row, east)),
        (edge.at[0, pl.ds(0, 2)], hcor.at[3], (up, west)),
        (edge.at[1, pl.ds(0, 2)], hcor.at[2], (up, east)),
        (edge.at[0, pl.ds(14, 2)], hcor.at[1], (down, west)),
        (edge.at[1, pl.ds(14, 2)], hcor.at[0], (down, east)),
    ]
    edge_copies = [
        pltpu.make_async_remote_copy(
            src_ref=src, dst_ref=dst, send_sem=edge_send.at[i], recv_sem=edge_recv.at[i],
            device_id=there, device_id_type=MESH,
        )
        for i, (src, dst, there) in enumerate(moves)
    ]
    for copy in edge_copies:
        copy.start()
    ring_tell(0)

    part_copies = []
    for k, copy in spec_copies:
        copy.wait()
        part[k] = jnp.dot(srf_ref[...], spec[k], preferred_element_type=F32)
        if k:
            out = pltpu.make_async_remote_copy(
                src_ref=part.at[k], dst_ref=gains.at[k], send_sem=part_send.at[k], recv_sem=part_recv.at[k],
                device_id=(row, lax.rem(col + k, N_COL)), device_id_type=MESH,
            )
            out.start()
            part_copies.append(out)

    w_ref[0] = jnp.zeros((256, 128), BF16)
    w_ref[KS + 1] = jnp.zeros((256, 128), BF16)

    tap = lax.broadcasted_iota(jnp.int32, (128, 256), 0)
    at = lax.broadcasted_iota(jnp.int32, (128, 256), 1)
    flip = jnp.where((tap + at == 256) | ((tap == 0) & (at == 0)), 1.0, 0.0).astype(BF16)
    lines[...] = jnp.dot(taps[...], flip, preferred_element_type=F32)

    def band(a, carry):
        line = jnp.broadcast_to(lines[pl.ds(a, 1), :], (256, 256))
        w_ref[a + 1] = pltpu.roll(line, 0, 1, stride=1, stride_axis=0)[:, :128].astype(BF16)
        return carry

    lax.fori_loop(0, KS, band, 0)

    blank = jnp.zeros((BANDS, 128), F32)

    def shifted(cells):
        return pltpu.roll(jnp.concatenate([cells.astype(F32), blank], axis=1), EDGE, 1)

    def lay(g, carry):
        for k in range(8):
            y = k + EDGE
            p_ref[4 * g + y // 2, y % 2] = shifted(own[8 * g + k]).astype(BF16)
        return carry

    lax.fori_loop(0, TR // 8, lay, 0)
    p_ref[73, 0] = jnp.zeros((BANDS, 640), BF16)
    p_ref[73, 1] = jnp.zeros((BANDS, 640), BF16)

    for copy in edge_copies:
        copy.wait_recv()
    ring_hear(0)
    ring_tell(1)

    has_up, has_down = row > 0, row < N_ROW - 1
    has_west, has_east = col > 0, col < N_COL - 1

    def west_side(packed, k, tile, keep):
        piece = packed.astype(F32)
        piece = pltpu.roll(piece, 128 - 16 * k, 1) if k else piece
        return jnp.where(lane < EDGE, jnp.where(keep, piece, 0.0), tile)

    def east_side(packed, k, tile, keep):
        piece = pltpu.roll(packed.astype(F32), (128 + EDGE - 16 * k) % 128, 1)
        return jnp.where((lane >= EDGE) & (lane < 2 * EDGE), jnp.where(keep, piece, 0.0), tile)

    def sides(g, carry):
        for k in range(8):
            y = k + EDGE
            at = (4 * g + y // 2, y % 2)
            p_ref[at[0], at[1], :, 0:128] = west_side(
                hcol[0, g], k, p_ref[at[0], at[1], :, 0:128].astype(F32), has_west
            ).astype(BF16)
            p_ref[at[0], at[1], :, TC : TC + 128] = east_side(
                hcol[1, g], k, p_ref[at[0], at[1], :, TC : TC + 128].astype(F32), has_east
            ).astype(BF16)
        return carry

    lax.fori_loop(0, TR // 8, sides, 0)
    for half, first, keep in ((0, 8 - 1, has_up), (1, 0, has_down)):
        for i in range(EDGE):
            y = i if half == 0 else TR + EDGE + i
            g, k = (first + i) // 8, (first + i) % 8
            line = shifted(jnp.where(keep, hrow[half, i].astype(F32), 0.0))
            west_tile = west_side(hcor[2 * half, g], k, line[:, :128], keep & has_west)
            east_tile = east_side(hcor[2 * half + 1, g], k, line[:, TC:], keep & has_east)
            whole = jnp.concatenate([west_tile, line[:, 128:TC], east_tile], axis=1)
            p_ref[y // 2, y % 2] = whole.astype(BF16)

    def products(yb):
        total = None
        for a in range(KS + 1):
            left = jnp.concatenate(
                [
                    p_ref[pl.ds(yb * 8 + a // 2, 8), a % 2, :, j * 128 : j * 128 + 256].reshape(128, 256)
                    for j in range(4)
                ],
                axis=0,
            )
            right = jnp.concatenate([w_ref[a + 1], w_ref[a]], axis=1)
            term = jnp.dot(left, right, preferred_element_type=F32)
            total = term if total is None else total + term
        return total

    def settle(yb):
        kept = accb[...].astype(BF16)
        rounded = kept.astype(F32)
        for j in range(4):
            strips = []
            for m in range(8):
                for q in range(2):
                    part_of = (slice(j * 128 + m * 16, j * 128 + m * 16 + 16), slice(q * 128, q * 128 + 128))
                    strips.append(rounded[part_of])
                    own[yb * 16 + 2 * m + q, :, j * 128 : j * 128 + 128] = kept[part_of]
            for h in range(2):
                cells = jnp.transpose(jnp.concatenate(strips[8 * h : 8 * h + 8], axis=0))
                for t in range(UNITS):
                    at = pl.multiple_of(t * CELLS + (2 * yb + h) * TC + j * 128, 128)
                    rot[pl.ds(at, 128), :] = pltpu.roll(cells, 16 * t, 1) if t else cells

    accb[...] = products(0)
    for copy in edge_copies:
        copy.wait_send()
    ring_hear(1)
    ring_tell(2)

    def block(yb, carry):
        settle(yb - 1)
        accb[...] = products(yb)
        return carry

    lax.fori_loop(1, 3, block, 0)
    ring_hear(2)
    ring_tell(3)
    lax.fori_loop(3, TR // 16, block, 0)
    ring_hear(3)
    settle(TR // 16 - 1)
    out_copy = pltpu.make_async_copy(own, blur_out, out_sem)
    out_copy.start()
    foot_copy.wait()

    stage[...] = jnp.zeros(stage.shape, F32)
    acc[...] = jnp.zeros(acc.shape, F32)
    lane8 = lax.broadcasted_iota(jnp.int32, (UNITS, 128), 1)

    def gather(g):
        for k in range(CAP):
            u, r = k // ROWS, k % ROWS
            lanes = slice(16 * u, 16 * u + 16)
            stage[g, r : r + 1, lanes] = rot[pl.ds(sm[g, 0, k], 1), lanes]
        return stage[g].astype(BF16)

    def message(n, mark):
        return pltpu.make_async_remote_copy(
            src_ref=send.at[n], dst_ref=recv.at[n], send_sem=send_sem, recv_sem=recv_sem.at[mark],
            device_id=place(lax.rem(me + n, ND)), device_id_type=MESH,
        )

    def arrived(n, count, mark):
        pltpu.make_async_copy(send.at[pl.ds(n, count)], recv.at[pl.ds(n, count)], recv_sem.at[mark]).wait()

    def add_up(steps):
        blocks = [recv[n].astype(F32) for n in steps]
        blocks.append(jnp.zeros((128 - PADR * len(steps), 128), F32))
        foot = jnp.full((UNITS, 128), FPD, jnp.int32)
        for g, n in enumerate(steps):
            feet = foot_ref[lax.rem(me + ND - n, ND)]
            inside = (lane8 >= PADR * g) & (lane8 < PADR * g + PADR)
            foot = jnp.where(inside, pltpu.roll(feet, PADR * g, 1) if g else feet, foot)
        cols = jnp.transpose(jnp.concatenate(blocks, axis=0))
        masked, low = [], []
        for u in range(UNITS):
            hi = jnp.broadcast_to(lax.shift_right_logical(foot[u : u + 1], 7), (BANDS, 128))
            lo = jnp.broadcast_to(foot[u : u + 1] & 127, (128, 128))
            vals = cols[16 * u : 16 * u + 16]
            masked.append(
                jnp.concatenate([jnp.where(hi == h, vals, 0.0) for h in range(HI)], axis=0).astype(BF16)
            )
            hit = lo == lax.broadcasted_iota(jnp.int32, (128, 128), 0)
            low.append(jnp.where(hit, 1.0, 0.0).astype(BF16))
        acc[...] += lax.dot_general(
            jnp.concatenate(masked, axis=1),
            jnp.concatenate(low, axis=1),
            (((1,), (1,)), ((), ())),
            preferred_element_type=F32,
        )

    for g, n in ((0, 0), (1, ND - 1)):
        fetch(n, g).wait()
        if n:
            send[n] = gather(g)
            message(n, TRIOS).start()
        else:
            recv[0] = gather(g)
        fetch(step_of(g + SLOTS), g).start()

    def sums(first, waiting):
        trio = lax.div(first, 3)
        if waiting:
            arrived(first, 3, trio)
            arrived(first + 3, 3, trio + 1)
        add_up([first, first + 1, first + 2])
        add_up([first + 3, first + 4, first + 5])

    def segment(n, slots, summing):
        trio = lax.div(n, 3)
        for k, g in enumerate(slots):
            fetch(n + k, g).wait()
        if summing:
            sums(n - BATCH * LAG, True)
        for k, g in enumerate(slots):
            send[n + k] = gather(g)
        for k, g in enumerate(slots):
            fetch(jnp.minimum(n + k + SLOTS, ND - 1), g).start()
        for k in range(BATCH):
            message(n + k, trio + k // 3).start()

    early = tuple(range(2, 2 + BATCH))
    late = tuple((2 + BATCH + k) % SLOTS for k in range(BATCH))

    def turns(summing):
        def turn(i, carry):
            n = 1 + 2 * BATCH * i
            segment(n, early, summing)
            segment(n + BATCH, late, summing)
            return carry

        return turn

    lax.fori_loop(0, LAG // 2, turns(False), 0)
    lax.fori_loop(LAG // 2, TRIPS, turns(True), 0)
    segment(1 + 2 * BATCH * TRIPS, early, True)

    def rest(i, carry):
        sums(1 + BATCH * i, True)
        return carry

    lax.fori_loop(2 * TRIPS + 1 - LAG, 2 * TRIPS + 1, rest, 0)
    arrived(ND - 1, 1, TRIOS)
    add_up([0, ND - 1])

    for copy in part_copies:
        copy.wait_recv()
    for h in range(HI):
        lanes = slice(128 * h, 128 * h + 128)
        evolved = part[0, :, lanes]
        for k in range(1, N_COL):
            evolved = evolved + gains[k, :, lanes]
        miss_out[:, lanes] = evolved - acc[16 * h : 16 * h + 16, :] * (1.0 / NSAMP)

    for g in range(SLOTS):
        fetch(0, g).wait()
    for copy in part_copies:
        copy.wait_send()
    out_copy.wait()
    pltpu.make_async_copy(send.at[pl.ds(1, ND - 1)], recv.at[pl.ds(1, ND - 1)], send_sem).wait()


def body(disk, response, spectra, srf, send_pix, recv_foot):
    vmem = pl.BlockSpec(memory_space=pltpu.VMEM)
    hbm = pl.BlockSpec(memory_space=pl.ANY)

    turned = jnp.transpose(disk, (1, 0, 2))
    taps = jnp.pad(response, ((0, 24 - KS), (0, 128 - KS)))

    pix = jnp.pad(send_pix.reshape(ND, 1, CAP), ((0, 0), (0, 0), (0, 384 - CAP)))
    slot = lax.broadcasted_iota(jnp.int32, pix.shape, 2) // ROWS
    idx = (((slot - (pix >> 9)) & 7) << 13) | ((pix >> 12) << 9) | (pix & 511)

    foot = recv_foot.reshape(ND, UNITS, ROWS)
    foot = jnp.pad(foot, ((0, 0), (0, 0), (0, 128 - ROWS)), constant_values=FPD)

    dma = pltpu.SemaphoreType.DMA
    blurred, mismatch = pl.pallas_call(
        kernel,
        out_shape=(
            jax.ShapeDtypeStruct((TR, BANDS, TC), BF16),
            jax.ShapeDtypeStruct((BANDS, FPD), F32),
        ),
        in_specs=[hbm, vmem, vmem, hbm, hbm, hbm],
        out_specs=(hbm, vmem),
        scratch_shapes=[
            pltpu.VMEM((TR, BANDS, TC), BF16),
            pltpu.VMEM((74, 2, BANDS, 640), BF16),
            pltpu.VMEM((KS + 2, 256, 128), BF16),
            pltpu.VMEM((24, 256), F32),
            pltpu.VMEM((N_COL, 512, FPD), BF16),
            pltpu.VMEM((N_COL, BANDS, FPD), F32),
            pltpu.VMEM((N_COL, BANDS, FPD), F32),
            pltpu.VMEM((2, 16, BANDS, 128), BF16),
            pltpu.VMEM((2, EDGE, BANDS, TC), BF16),
            pltpu.VMEM((2, 16, BANDS, 128), BF16),
            pltpu.VMEM((4, 2, BANDS, 128), BF16),
            pltpu.VMEM((512, 256), F32),
            pltpu.VMEM((ND, UNITS, 128), jnp.int32),
            pltpu.VMEM((UNITS * CELLS, 128), F32),
            pltpu.VMEM((SLOTS, PADR, 128), F32),
            pltpu.VMEM((ND, PADR, 128), BF16),
            pltpu.VMEM((ND, PADR, 128), BF16),
            pltpu.VMEM((HI * BANDS, 128), F32),
            pltpu.SMEM((SLOTS, 1, 384), jnp.int32),
            pltpu.SemaphoreType.REGULAR((4,)),
            dma,
            dma,
            dma,
            dma((N_COL,)),
            dma((SLOTS,)),
            dma((8,)),
            dma((8,)),
            dma((N_COL,)),
            dma((N_COL,)),
            dma,
            dma((TRIOS + 1,)),
        ],
        compiler_params=pltpu.CompilerParams(
            vmem_limit_bytes=60 << 20, collective_id=0, has_side_effects=True
        ),
        cost_estimate=pl.CostEstimate(flops=16 << 30, bytes_accessed=16 << 20, transcendentals=0),
        name="collocate",
    )(turned, taps, srf, spectra, idx, foot)
    return jnp.transpose(blurred, (1, 0, 2)), mismatch


def solution(mesh):
    placed = (
        P(None, "row", "col"),
        P(),
        P("col", "row"),
        P(None, "col"),
        P(("row", "col")),
        P(("row", "col")),
    )
    return jax.shard_map(
        body,
        mesh=mesh,
        in_specs=placed,
        out_specs=(P(None, "row", "col"), P(None, ("row", "col"))),
        check_vma=False,
    )
```

```python
import jax
import jax.numpy as jnp
from jax import lax
from jax.experimental import pallas as pl
from jax.experimental.pallas import tpu as pltpu
from jax.sharding import PartitionSpec as P

NSAMP = 16
BANDS = 16
KS = 19
EDGE = KS // 2
TR = 128
TC = 512
FPD = 1536
ND = 128
N_ROW = 32
N_COL = 4
CAP = 288
UNITS = 8
ROWS = CAP // UNITS
PADR = 40
CELLS = TR // 8 * TC
HI = FPD // 128
BATCH = 6
SLOTS = 2 * BATCH
TRIPS = 10
LAG = 10
TRIOS = 2 * (2 * TRIPS + 1)
MESH = pl.DeviceIdType.MESH
F32 = jnp.float32
BF16 = jnp.bfloat16


def kernel(
    turned, taps, srf_ref, spectra, idx_ref, feet, blur_out, miss_out,
    own, p_ref, w_ref, lines, spec, part, gains, edge, hrow, hcol, hcor, accb, foot_ref, rot, stage, send, recv,
    acc, sm, ring, own_sem, out_sem, foot_sem, spec_sem, idx_sem, edge_send, edge_recv, part_send, part_recv, send_sem, recv_sem,
):
    row = lax.axis_index("row")
    col = lax.axis_index("col")
    me = row * N_COL + col

    def place(d):
        r = lax.div(d, N_COL)
        return (r, d - r * N_COL)

    own_copy = pltpu.make_async_copy(turned, own, own_sem)
    own_copy.start()
    foot_copy = pltpu.make_async_copy(feet, foot_ref, foot_sem)
    foot_copy.start()
    spec_copies = []
    for k in (1, 2, 3, 0):
        at = pl.multiple_of(lax.rem(col + k, N_COL) * FPD, 128)
        copy = pltpu.make_async_copy(spectra.at[:, pl.ds(at, FPD)], spec.at[k], spec_sem.at[k])
        copy.start()
        spec_copies.append((k, copy))

    def step_of(q):
        return q - 1

    def fetch(n, g):
        return pltpu.make_async_copy(idx_ref.at[lax.rem(me + n, ND)], sm.at[g], idx_sem.at[g])

    for g in range(SLOTS):
        fetch((0, ND - 1)[g] if g < 2 else step_of(g), g).start()

    def around(value, by, count):
        moved = value + by
        return jnp.where(moved >= count, moved - count, jnp.where(moved < 0, moved + count, moved))

    barrier = pltpu.get_barrier_semaphore()
    for dr, dc in [(0, 1), (0, 2), (0, 3)] + [(dr, dc) for dr in (1, -1) for dc in range(N_COL)]:
        there = (around(row, dr, N_ROW), around(col, dc, N_COL))
        pl.semaphore_signal(barrier, inc=1, device_id=there, device_id_type=MESH)

    def ring_tell(level):
        for by in (1 << level, -(1 << level)):
            pl.semaphore_signal(
                ring.at[level], inc=1, device_id=(around(row, by, N_ROW), col), device_id_type=MESH
            )

    def ring_hear(level):
        pl.semaphore_wait(ring.at[level], 2)

    lane = lax.broadcasted_iota(jnp.int32, (BANDS, 128), 1)
    own_copy.wait()

    def pack(g, carry):
        left = jnp.zeros((BANDS, 128), F32)
        right = jnp.zeros((BANDS, 128), F32)
        for k in range(8):
            a = own[8 * g + k, :, 0:128].astype(F32)
            b = own[8 * g + k, :, TC - 128 : TC].astype(F32)
            left = jnp.where(lane // 16 == k, pltpu.roll(a, 16 * k, 1) if k else a, left)
            right = jnp.where(lane // 16 == k, pltpu.roll(b, (16 * k + EDGE) % 128, 1), right)
        edge[0, g] = left.astype(BF16)
        edge[1, g] = right.astype(BF16)
        return carry

    lax.fori_loop(0, TR // 8, pack, 0)
    pl.semaphore_wait(barrier, 2 * N_COL + N_COL - 1)

    up, down = lax.rem(row + N_ROW - 1, N_ROW), lax.rem(row + 1, N_ROW)
    west, east = lax.rem(col + N_COL - 1, N_COL), lax.rem(col + 1, N_COL)
    moves = [
        (own.at[pl.ds(0, EDGE)], hrow.at[1], (up, col)),
        (own.at[pl.ds(TR - EDGE, EDGE)], hrow.at[0], (down, col)),
        (edge.at[0], hcol.at[1], (row, west)),
        (edge.at[1], hcol.at[0], (row, east)),
        (edge.at[0, pl.ds(0, 2)], hcor.at[3], (up, west)),
        (edge.at[1, pl.ds(0, 2)], hcor.at[2], (up, east)),
        (edge.at[0, pl.ds(14, 2)], hcor.at[1], (down, west)),
        (edge.at[1, pl.ds(14, 2)], hcor.at[0], (down, east)),
    ]
    edge_copies = [
        pltpu.make_async_remote_copy(
            src_ref=src, dst_ref=dst, send_sem=edge_send.at[i], recv_sem=edge_recv.at[i],
            device_id=there, device_id_type=MESH,
        )
        for i, (src, dst, there) in enumerate(moves)
    ]
    for copy in edge_copies:
        copy.start()
    ring_tell(0)

    part_copies = []
    for k, copy in spec_copies:
        copy.wait()
        part[k] = jnp.dot(srf_ref[...], spec[k], preferred_element_type=F32)
        if k:
            out = pltpu.make_async_remote_copy(
                src_ref=part.at[k], dst_ref=gains.at[k], send_sem=part_send.at[k], recv_sem=part_recv.at[k],
                device_id=(row, lax.rem(col + k, N_COL)), device_id_type=MESH,
            )
            out.start()
            part_copies.append(out)

    w_ref[0] = jnp.zeros((256, 128), BF16)
    w_ref[KS + 1] = jnp.zeros((256, 128), BF16)

    tap = lax.broadcasted_iota(jnp.int32, (KS, 256), 0)
    at = lax.broadcasted_iota(jnp.int32, (KS, 256), 1)
    flip = jnp.where((tap + at == 256) | ((tap == 0) & (at == 0)), 1.0, 0.0).astype(BF16)
    lines[0:KS, :] = jnp.dot(taps[...], flip, preferred_element_type=F32)

    def band(a, carry):
        line = jnp.broadcast_to(lines[pl.ds(a, 1), :], (256, 256))
        w_ref[a + 1] = pltpu.roll(line, 0, 1, stride=1, stride_axis=0)[:, :128].astype(BF16)
        return carry

    lax.fori_loop(0, KS, band, 0)

    blank = jnp.zeros((BANDS, 128), F32)

    def shifted(cells):
        return pltpu.roll(jnp.concatenate([cells.astype(F32), blank], axis=1), EDGE, 1)

    def lay(g, carry):
        for k in range(8):
            y = k + EDGE
            p_ref[4 * g + y // 2, y % 2] = shifted(own[8 * g + k]).astype(BF16)
        return carry

    lax.fori_loop(0, TR // 8, lay, 0)
    p_ref[73, 0] = jnp.zeros((BANDS, 640), BF16)
    p_ref[73, 1] = jnp.zeros((BANDS, 640), BF16)

    for copy in edge_copies:
        copy.wait_recv()
    ring_hear(0)
    ring_tell(1)

    has_up, has_down = row > 0, row < N_ROW - 1
    has_west, has_east = col > 0, col < N_COL - 1

    def west_side(packed, k, tile, keep):
        piece = packed.astype(F32)
        piece = pltpu.roll(piece, 128 - 16 * k, 1) if k else piece
        return jnp.where(lane < EDGE, jnp.where(keep, piece, 0.0), tile)

    def east_side(packed, k, tile, keep):
        piece = pltpu.roll(packed.astype(F32), (128 + EDGE - 16 * k) % 128, 1)
        return jnp.where((lane >= EDGE) & (lane < 2 * EDGE), jnp.where(keep, piece, 0.0), tile)

    def sides(g, carry):
        for k in range(8):
            y = k + EDGE
            at = (4 * g + y // 2, y % 2)
            p_ref[at[0], at[1], :, 0:128] = west_side(
                hcol[0, g], k, p_ref[at[0], at[1], :, 0:128].astype(F32), has_west
            ).astype(BF16)
            p_ref[at[0], at[1], :, TC : TC + 128] = east_side(
                hcol[1, g], k, p_ref[at[0], at[1], :, TC : TC + 128].astype(F32), has_east
            ).astype(BF16)
        return carry

    lax.fori_loop(0, TR // 8, sides, 0)
    for half, first, keep in ((0, 8 - 1, has_up), (1, 0, has_down)):
        for i in range(EDGE):
            y = i if half == 0 else TR + EDGE + i
            g, k = (first + i) // 8, (first + i) % 8
            line = shifted(jnp.where(keep, hrow[half, i].astype(F32), 0.0))
            west_tile = west_side(hcor[2 * half, g], k, line[:, :128], keep & has_west)
            east_tile = east_side(hcor[2 * half + 1, g], k, line[:, TC:], keep & has_east)
            whole = jnp.concatenate([west_tile, line[:, 128:TC], east_tile], axis=1)
            p_ref[y // 2, y % 2] = whole.astype(BF16)

    def products(yb):
        total = None
        for a in range(KS + 1):
            left = jnp.concatenate(
                [
                    p_ref[pl.ds(yb * 8 + a // 2, 8), a % 2, :, j * 128 : j * 128 + 256].reshape(128, 256)
                    for j in range(4)
                ],
                axis=0,
            )
            right = jnp.concatenate([w_ref[a + 1], w_ref[a]], axis=1)
            term = jnp.dot(left, right, preferred_element_type=F32)
            total = term if total is None else total + term
        return total

    def settle(yb):
        kept = accb[...].astype(BF16)
        rounded = kept.astype(F32)
        for j in range(4):
            strips = []
            for m in range(8):
                for q in range(2):
                    part_of = (slice(j * 128 + m * 16, j * 128 + m * 16 + 16), slice(q * 128, q * 128 + 128))
                    strips.append(rounded[part_of])
                    own[yb * 16 + 2 * m + q, :, j * 128 : j * 128 + 128] = kept[part_of]
            for h in range(2):
                cells = jnp.transpose(jnp.concatenate(strips[8 * h : 8 * h + 8], axis=0))
                for t in range(UNITS):
                    at = pl.multiple_of(t * CELLS + (2 * yb + h) * TC + j * 128, 128)
                    rot[pl.ds(at, 128), :] = pltpu.roll(cells, 16 * t, 1) if t else cells

    accb[...] = products(0)
    for copy in edge_copies:
        copy.wait_send()
    ring_hear(1)
    ring_tell(2)

    def block(yb, carry):
        settle(yb - 1)
        accb[...] = products(yb)
        return carry

    lax.fori_loop(1, 3, block, 0)
    ring_hear(2)
    ring_tell(3)
    lax.fori_loop(3, TR // 16, block, 0)
    ring_hear(3)
    settle(TR // 16 - 1)
    out_copy = pltpu.make_async_copy(own, blur_out, out_sem)
    out_copy.start()
    foot_copy.wait()

    stage[...] = jnp.zeros(stage.shape, F32)
    acc[...] = jnp.zeros(acc.shape, F32)
    lane8 = lax.broadcasted_iota(jnp.int32, (UNITS, 128), 1)

    def gather(g):
        for k in range(CAP):
            u, r = k // ROWS, k % ROWS
            lanes = slice(16 * u, 16 * u + 16)
            stage[g, r : r + 1, lanes] = rot[pl.ds(sm[g, 0, k], 1), lanes]
        return stage[g].astype(BF16)

    def message(n, mark):
        return pltpu.make_async_remote_copy(
            src_ref=send.at[n], dst_ref=recv.at[n], send_sem=send_sem, recv_sem=recv_sem.at[mark],
            device_id=place(lax.rem(me + n, ND)), device_id_type=MESH,
        )

    def arrived(n, count, mark):
        pltpu.make_async_copy(send.at[pl.ds(n, count)], recv.at[pl.ds(n, count)], recv_sem.at[mark]).wait()

    def add_up(steps):
        blocks = [recv[n].astype(F32) for n in steps]
        blocks.append(jnp.zeros((128 - PADR * len(steps), 128), F32))
        foot = jnp.full((UNITS, 128), FPD, jnp.int32)
        for g, n in enumerate(steps):
            feet = foot_ref[lax.rem(me + ND - n, ND)]
            inside = (lane8 >= PADR * g) & (lane8 < PADR * g + PADR)
            foot = jnp.where(inside, pltpu.roll(feet, PADR * g, 1) if g else feet, foot)
        cols = jnp.transpose(jnp.concatenate(blocks, axis=0))
        masked, low = [], []
        for u in range(UNITS):
            hi = jnp.broadcast_to(lax.shift_right_logical(foot[u : u + 1], 7), (BANDS, 128))
            lo = jnp.broadcast_to(foot[u : u + 1] & 127, (128, 128))
            vals = cols[16 * u : 16 * u + 16]
            masked.append(
                jnp.concatenate([jnp.where(hi == h, vals, 0.0) for h in range(HI)], axis=0).astype(BF16)
            )
            hit = lo == lax.broadcasted_iota(jnp.int32, (128, 128), 0)
            low.append(jnp.where(hit, 1.0, 0.0).astype(BF16))
        acc[...] += lax.dot_general(
            jnp.concatenate(masked, axis=1),
            jnp.concatenate(low, axis=1),
            (((1,), (1,)), ((), ())),
            preferred_element_type=F32,
        )

    for g, n in ((0, 0), (1, ND - 1)):
        fetch(n, g).wait()
        if n:
            send[n] = gather(g)
            message(n, TRIOS).start()
        else:
            recv[0] = gather(g)
        fetch(step_of(g + SLOTS), g).start()

    def sums(first, waiting):
        trio = lax.div(first, 3)
        if waiting:
            arrived(first, 3, trio)
            arrived(first + 3, 3, trio + 1)
        add_up([first, first + 1, first + 2])
        add_up([first + 3, first + 4, first + 5])

    def segment(n, slots, summing):
        trio = lax.div(n, 3)
        for k, g in enumerate(slots):
            fetch(n + k, g).wait()
        if summing:
            sums(n - BATCH * LAG, True)
        for k, g in enumerate(slots):
            send[n + k] = gather(g)
        for k, g in enumerate(slots):
            fetch(jnp.minimum(n + k + SLOTS, ND - 1), g).start()
        for k in range(BATCH):
            message(n + k, trio + k // 3).start()

    early = tuple(range(2, 2 + BATCH))
    late = tuple((2 + BATCH + k) % SLOTS for k in range(BATCH))

    def turns(summing):
        def turn(i, carry):
            n = 1 + 2 * BATCH * i
            segment(n, early, summing)
            segment(n + BATCH, late, summing)
            return carry

        return turn

    lax.fori_loop(0, LAG // 2, turns(False), 0)
    lax.fori_loop(LAG // 2, TRIPS, turns(True), 0)
    segment(1 + 2 * BATCH * TRIPS, early, True)

    def rest(i, carry):
        sums(1 + BATCH * i, True)
        return carry

    lax.fori_loop(2 * TRIPS + 1 - LAG, 2 * TRIPS + 1, rest, 0)
    arrived(ND - 1, 1, TRIOS)
    add_up([0, ND - 1])

    for copy in part_copies:
        copy.wait_recv()
    for h in range(HI):
        lanes = slice(128 * h, 128 * h + 128)
        evolved = part[0, :, lanes]
        for k in range(1, N_COL):
            evolved = evolved + gains[k, :, lanes]
        miss_out[:, lanes] = evolved - acc[16 * h : 16 * h + 16, :] * (1.0 / NSAMP)

    for g in range(SLOTS):
        fetch(0, g).wait()
    for copy in part_copies:
        copy.wait_send()
    out_copy.wait()
    pltpu.make_async_copy(send.at[pl.ds(1, ND - 1)], recv.at[pl.ds(1, ND - 1)], send_sem).wait()


def body(disk, response, spectra, srf, send_pix, recv_foot):
    vmem = pl.BlockSpec(memory_space=pltpu.VMEM)
    hbm = pl.BlockSpec(memory_space=pl.ANY)

    turned = jnp.transpose(disk, (1, 0, 2))
    pix = jnp.pad(send_pix.reshape(ND, 1, CAP), ((0, 0), (0, 0), (0, 384 - CAP)))
    slot = lax.broadcasted_iota(jnp.int32, pix.shape, 2) // ROWS
    idx = (((slot - (pix >> 9)) & 7) << 13) | ((pix >> 12) << 9) | (pix & 511)

    foot = recv_foot.reshape(ND, UNITS, ROWS)
    foot = jnp.pad(foot, ((0, 0), (0, 0), (0, 128 - ROWS)), constant_values=FPD)

    dma = pltpu.SemaphoreType.DMA
    blurred, mismatch = pl.pallas_call(
        kernel,
        out_shape=(
            jax.ShapeDtypeStruct((TR, BANDS, TC), BF16),
            jax.ShapeDtypeStruct((BANDS, FPD), F32),
        ),
        in_specs=[hbm, vmem, vmem, hbm, hbm, hbm],
        out_specs=(hbm, vmem),
        scratch_shapes=[
            pltpu.VMEM((TR, BANDS, TC), BF16),
            pltpu.VMEM((74, 2, BANDS, 640), BF16),
            pltpu.VMEM((KS + 2, 256, 128), BF16),
            pltpu.VMEM((24, 256), F32),
            pltpu.VMEM((N_COL, 512, FPD), BF16),
            pltpu.VMEM((N_COL, BANDS, FPD), F32),
            pltpu.VMEM((N_COL, BANDS, FPD), F32),
            pltpu.VMEM((2, 16, BANDS, 128), BF16),
            pltpu.VMEM((2, EDGE, BANDS, TC), BF16),
            pltpu.VMEM((2, 16, BANDS, 128), BF16),
            pltpu.VMEM((4, 2, BANDS, 128), BF16),
            pltpu.VMEM((512, 256), F32),
            pltpu.VMEM((ND, UNITS, 128), jnp.int32),
            pltpu.VMEM((UNITS * CELLS, 128), F32),
            pltpu.VMEM((SLOTS, PADR, 128), F32),
            pltpu.VMEM((ND, PADR, 128), BF16),
            pltpu.VMEM((ND, PADR, 128), BF16),
            pltpu.VMEM((HI * BANDS, 128), F32),
            pltpu.SMEM((SLOTS, 1, 384), jnp.int32),
            pltpu.SemaphoreType.REGULAR((4,)),
            dma,
            dma,
            dma,
            dma((N_COL,)),
            dma((SLOTS,)),
            dma((8,)),
            dma((8,)),
            dma((N_COL,)),
            dma((N_COL,)),
            dma,
            dma((TRIOS + 1,)),
        ],
        compiler_params=pltpu.CompilerParams(
            vmem_limit_bytes=60 << 20, collective_id=0, has_side_effects=True
        ),
        cost_estimate=pl.CostEstimate(flops=16 << 30, bytes_accessed=16 << 20, transcendentals=0),
        name="collocate",
    )(turned, response, srf, spectra, idx, foot)
    return jnp.transpose(blurred, (1, 0, 2)), mismatch


def solution(mesh):
    placed = (
        P(None, "row", "col"),
        P(),
        P("col", "row"),
        P(None, "col"),
        P(("row", "col")),
        P(("row", "col")),
    )
    return jax.shard_map(
        body,
        mesh=mesh,
        in_specs=placed,
        out_specs=(P(None, "row", "col"), P(None, ("row", "col"))),
        check_vma=False,
    )
```
